32 devices in a mesh: groups: 2 (over y), seq: 16 (over z, x, core).
Axes of the slice: x: 2, y: 2, z: 4, core: 2. Of those that a mesh axis runs over, the one named last changes fastest.
Arguments:
- video_q: bfloat16 [8192, 1536], P(('groups', 'seq')), parts along dimension 0, may hold values from -9 to 9
- video_k: bfloat16 [8192, 1536], P(('groups', 'seq')), parts along dimension 0, may hold values from -9 to 9
- video_v: bfloat16 [8192, 1536], P(('groups', 'seq')), parts along dimension 0, may hold values from -6 to 6
- audio_query_rows: bfloat16 [2048, 1536], P(('groups', 'seq')), parts along dimension 0, may hold values from -9 to 9
- audio_k: bfloat16 [2048, 1536], P(('groups', 'seq')), parts along dimension 0, may hold values from -9 to 9
- audio_v: bfloat16 [2048, 1536], P(('groups', 'seq')), parts along dimension 0, may hold values from -6 to 6
- video_start: int32 [32], P(('groups', 'seq')), parts along dimension 0, may hold values from 0 to 15, as said below
- video_count: int32 [32], P(('groups', 'seq')), parts along dimension 0, may hold values from 1 to 5, as said below
- audio_start: int32 [32], P(('groups', 'seq')), parts along dimension 0, may hold values from 0 to 15, as said below
- audio_count: int32 [32], P(('groups', 'seq')), parts along dimension 0, may hold values from 1 to 5, as said below
Outputs:
- video_out: bfloat16 [8192, 1536], P(('groups', 'seq')), parts along dimension 0
- audio_out: bfloat16 [2048, 1536], P(('groups', 'seq')), parts along dimension 0
The draws below stay inside these ranges and needn't reach their ends.
There are 2 independent parts, one for each index of `groups`. The reference program is written for one: setup_inputs(seed, part) draws one part's arguments, and reference() takes and returns one part's arrays. A program takes and returns all parts, laid end to end along the dimension named above; each array names one. Nothing has to cross between parts.
Inputs may be any that keep to these rules, and one draw needn't show every extreme that they name: `video_start`: video block i's band of audio blocks contains block i and lies within blocks i - 2 to i + 2. `video_count`: the band counts blocks within the clip; some video block's band holds 5 blocks. `audio_start`: audio block j's band of video blocks contains block j and lies within blocks j - 2 to j + 2. `audio_count`: the band counts blocks within the clip; some audio block's band holds 5 blocks.
All inputs are finite; a program needn't handle non-finite values.
Results may differ from the reference program's by a relative error of at most 0.0045.
Values may be sent and summed in bfloat16 or wider, within the bound.
No kernel may reach another device: no remote copies, remote signals or barrier semaphores. Data moves between devices by JAX's collectives and lax.ppermute only.
A program may use at most 64 MiB of HBM per device.

```python
import math
import jax
import jax.numpy as jnp
from jax import lax

HEADS = 12
HEAD_DIM = 128
RADIUS = 2
VTOK_DEV = 256
ATOK_DEV = 64
BLOCKS = 16
VTOKENS = 4096
ATOKENS = 1024


def fresh_rows(sub_key, row_total):
    features = HEADS * HEAD_DIM
    return jax.random.truncated_normal(sub_key, -6.0, 6.0, (row_total, features), jnp.float32)


def stream_tensors(key):
    branch_keys = jax.random.split(jax.random.fold_in(key, 17), 4)
    video_query = fresh_rows(branch_keys[0], VTOKENS)
    video_key = fresh_rows(branch_keys[1], VTOKENS)
    audio_query = fresh_rows(branch_keys[2], ATOKENS)
    audio_key = fresh_rows(branch_keys[3], ATOKENS)
    return (video_query, video_key, audio_query, audio_key)


def band_draw(key, salt_value):
    band_key = jax.random.fold_in(key, salt_value)
    key_left, key_right, key_widest = jax.random.split(band_key, 3)
    positions = jnp.arange(BLOCKS, dtype=jnp.int32)
    leftward_extent = jax.random.randint(key_left, (BLOCKS,), 0, RADIUS + 1, dtype=jnp.int32)
    reach_right = jax.random.randint(key_right, (BLOCKS,), 0, RADIUS + 1, dtype=jnp.int32)
    widest = jax.random.randint(key_widest, (), RADIUS, BLOCKS - RADIUS, dtype=jnp.int32)
    leftward_extent = jnp.where(positions == widest, RADIUS, leftward_extent)
    reach_right = jnp.where(positions == widest, RADIUS, reach_right)
    leftward_extent = jnp.where(positions == BLOCKS - 1, 0, leftward_extent)
    reach_right = jnp.where(positions == BLOCKS - 1, 0, reach_right)
    starts = jnp.maximum(positions - leftward_extent, 0)
    ends = jnp.minimum(positions + reach_right, BLOCKS - 1)
    return (starts.astype(jnp.int32), (ends - starts + 1).astype(jnp.int32))


def draw_video_q(key, part):
    return stream_tensors(key)[0].astype(jnp.bfloat16)


def draw_video_k(key, part):
    return stream_tensors(key)[1].astype(jnp.bfloat16)


def draw_audio_query_rows(key, part):
    return stream_tensors(key)[2].astype(jnp.bfloat16)


def draw_audio_k(key, part):
    return stream_tensors(key)[3].astype(jnp.bfloat16)


def draw_video_start(key, part):
    return band_draw(key, 101)[0]


def draw_video_count(key, part):
    return band_draw(key, 101)[1]


def draw_audio_start(key, part):
    return band_draw(key, 202)[0]


def draw_audio_count(key, part):
    return band_draw(key, 202)[1]


def block_scale(rng, shape, cuts, smallest, top_value):
    level, own = 1.0, jax.random.fold_in(rng, 6)
    for axis_at, shards_of in cuts:
        steps = jnp.exp(jax.random.uniform(jax.random.fold_in(own, axis_at), (shards_of,), jnp.float32, smallest / len(cuts), top_value / len(cuts)))
        level = level * jnp.repeat(steps, shape[axis_at] // shards_of).reshape([-1 if axis == axis_at else 1 for axis in range(len(shape))])
    return level


def gaussian(key, shape, spread, limit, cuts=(), kind=jnp.bfloat16):
    factor_of = block_scale(key, shape, cuts, -0.22, 0.18) if cuts else 1.0
    result = jax.random.normal(key, shape, jnp.float32) * spread * factor_of
    return jnp.minimum(jnp.maximum(result, -limit), limit).astype(kind)


def setup_inputs(seed: int = 0, part: int = 0) -> dict:
    streams_of = jax.random.split(jax.random.key(seed), 11)
    part_keys = jax.random.split(jax.random.fold_in(streams_of[10], part), 11)
    return {
        "video_q": draw_video_q(jax.random.fold_in(jax.random.fold_in(streams_of[10], part), 71), part),
        "video_k": draw_video_k(jax.random.fold_in(jax.random.fold_in(streams_of[10], part), 71), part),
        "video_v": gaussian(part_keys[2], (VTOKENS, HEADS * HEAD_DIM), 1.0, 6.0, ((0, 16),)),
        "audio_query_rows": draw_audio_query_rows(jax.random.fold_in(jax.random.fold_in(streams_of[10], part), 71), part),
        "audio_k": draw_audio_k(jax.random.fold_in(jax.random.fold_in(streams_of[10], part), 71), part),
        "audio_v": gaussian(part_keys[5], (ATOKENS, HEADS * HEAD_DIM), 1.0, 6.0, ((0, 16),)),
        "video_start": draw_video_start(jax.random.fold_in(jax.random.fold_in(streams_of[10], part), 71), part),
        "video_count": draw_video_count(jax.random.fold_in(jax.random.fold_in(streams_of[10], part), 71), part),
        "audio_start": draw_audio_start(jax.random.fold_in(jax.random.fold_in(streams_of[10], part), 71), part),
        "audio_count": draw_audio_count(jax.random.fold_in(jax.random.fold_in(streams_of[10], part), 71), part),
    }


def window_attend(queries, keys, values, starts, counts, q_rows, k_rows):
    features = queries.shape[1]
    window = 2 * RADIUS + 1
    padding = jnp.zeros((RADIUS * k_rows, features), keys.dtype)
    keys_pad = jnp.concatenate([padding, keys, padding], axis=0)
    values_pad = jnp.concatenate([padding, values, padding], axis=0)
    scale = 1.0 / math.sqrt(HEAD_DIM)

    def per_block(block_id):
        query_heads = lax.dynamic_slice_in_dim(queries, block_id * q_rows, q_rows, 0).astype(jnp.float32).reshape(q_rows, HEADS, HEAD_DIM)
        key_heads = lax.dynamic_slice_in_dim(keys_pad, block_id * k_rows, window * k_rows, 0).astype(jnp.float32).reshape(window, k_rows, HEADS, HEAD_DIM)
        value_heads = lax.dynamic_slice_in_dim(values_pad, block_id * k_rows, window * k_rows, 0).astype(jnp.float32).reshape(window, k_rows, HEADS, HEAD_DIM)
        scores = jnp.einsum('qhd,bkhd->hqbk', query_heads, key_heads) * scale
        maxima = lax.optimization_barrier(jnp.max(scores, axis=-1))
        raised = jnp.exp(scores - maxima[..., None])
        totals = lax.optimization_barrier(jnp.sum(raised, axis=-1))
        rounded = lax.optimization_barrier(raised.astype(jnp.bfloat16))
        numerators = jnp.einsum('hqbk,bkhd->qbhd', rounded.astype(jnp.float32), value_heads)
        nearby = block_id - RADIUS + jnp.arange(window, dtype=jnp.int32)
        band_start = starts[block_id]
        in_range = (nearby >= band_start) & (nearby < band_start + counts[block_id])
        highest = lax.optimization_barrier(jnp.max(jnp.where(in_range, maxima, -1e+30), axis=-1))
        weight = jnp.where(in_range, jnp.exp(maxima - highest[..., None]), 0.0)
        total_all = lax.optimization_barrier(jnp.sum(weight * totals, axis=-1))
        mixed = jnp.einsum('hqb,qbhd->qhd', weight, numerators) / total_all.T[:, :, None]
        return mixed.reshape(q_rows, HEADS * HEAD_DIM).astype(jnp.bfloat16)
    block_ids = jnp.arange(BLOCKS, dtype=jnp.int32)
    return lax.map(per_block, block_ids).reshape(BLOCKS * q_rows, features)

def reference(video_q, video_k, video_v, audio_query_rows, audio_k, audio_v, video_start, video_count, audio_start, audio_count):
    video_out = window_attend(video_q, audio_k, audio_v, video_start, video_count, VTOK_DEV, ATOK_DEV)
    audio_out = window_attend(audio_query_rows, video_k, video_v, audio_start, audio_count, ATOK_DEV, VTOK_DEV)
    return (video_out, audio_out)
```

```python
import functools
import math

import jax
import jax.numpy as jnp
from jax import lax
from jax.experimental import pallas as pl
from jax.experimental.pallas import tpu as pltpu
from jax.sharding import PartitionSpec as P

HEAD_DIM = 128
SCALE = math.log2(math.e) / math.sqrt(HEAD_DIM)
NEG = -1e30
BIG = 1e30

VMEM = pl.BlockSpec(memory_space=pltpu.VMEM)
SMEM = pl.BlockSpec(memory_space=pltpu.SMEM)


def pairs_of(n, to):
    pairs = [(s, to(s)) for s in range(n)]
    return [(s, d) for s, d in pairs if d is not None and 0 <= d < n]


def head_cols(h):
    return pl.ds(h * HEAD_DIM, HEAD_DIM)


def nt(a, b):
    return lax.dot_general(a, b, (((1,), (1,)), ((), ())), preferred_element_type=jnp.float32)


def nn(a, b):
    return lax.dot_general(a, b, (((1,), (0,)), ((), ())), preferred_element_type=jnp.float32)


def band_has(block, start, count):
    return (block >= start) & (block < start + count)


def lanes(shape):
    return lax.broadcasted_iota(jnp.int32, shape, len(shape) - 1)


def split3(x):
    hi = x.astype(jnp.bfloat16)
    rest = x - hi.astype(jnp.float32)
    mid = rest.astype(jnp.bfloat16)
    low = (rest - mid.astype(jnp.float32)).astype(jnp.bfloat16)
    return hi, mid, low


def guest_rows(q, k0, k1, v0, v1, in0, in1):
    s0, s1 = nt(q, k0), nt(q, k1)
    m0 = jnp.max(s0, axis=-1, keepdims=True) * SCALE
    m1 = jnp.max(s1, axis=-1, keepdims=True) * SCALE
    m = jnp.maximum(jnp.where(in0, m0, NEG), jnp.where(in1, m1, NEG))
    p0 = jnp.exp2(s0 * SCALE - jnp.where(in0, m, BIG))
    p1 = jnp.exp2(s1 * SCALE - jnp.where(in1, m, BIG))
    total = jnp.sum(p0, axis=-1, keepdims=True) + jnp.sum(p1, axis=-1, keepdims=True)
    total = jnp.maximum(total, 1.0)
    out = nn(p0.astype(jnp.bfloat16), v0) + nn(p1.astype(jnp.bfloat16), v1)
    return out / total, m + jnp.log2(total)


def store_guest(ret, base, heads, outs, stats):
    rows = ret.shape[0]
    lane = lanes((rows, HEAD_DIM))
    packed = jnp.zeros((rows, HEAD_DIM), jnp.float32)
    for h, st in enumerate(stats):
        for piece, val in enumerate(split3(st)):
            packed = jnp.where(lane == piece * 32 + h, val.astype(jnp.float32), packed)
    ret[:, pl.ds(heads * HEAD_DIM, HEAD_DIM)] = packed.astype(jnp.bfloat16)


def guests_kernel(heads, n, two, me, *refs):
    if two:
        start, count, code, qo, qx, k0, k1, v0, v1, own, own_stats, ret = refs
    else:
        code, qx, k0, k1, v0, v1, ret = refs
    me = me[0]
    mate = me ^ 1
    g_start, g_count = code[0] // 8, code[0] % 8
    rows = qx.shape[0]
    total_rows = 2 * rows if two else rows
    if two:
        first = lax.broadcasted_iota(jnp.int32, (total_rows, 1), 0) < rows
        lo = jnp.where(first, start[0], g_start)
        hi = lo + jnp.where(first, count[0], g_count)
    else:
        lo = jnp.full((total_rows, 1), g_start, jnp.int32)
        hi = lo + g_count
    in0 = (lo <= me) & (me < hi)
    in1 = (lo <= mate) & (mate < hi)
    stats = []
    lane = lanes((rows, HEAD_DIM))
    kept = jnp.zeros((rows, HEAD_DIM), jnp.float32)
    for h in range(heads):
        c = head_cols(h)
        q = jnp.concatenate([qo[:, c], qx[:, c]], axis=0) if two else qx[:, c]
        out, lse = guest_rows(q, k0[:, c], k1[:, c], v0[:, c], v1[:, c], in0, in1)
        if two:
            own[:, c] = out[:rows]
            kept = jnp.where(lane == h, lse[:rows], kept)
            out, lse = out[rows:], lse[rows:]
        ret[:, c] = out.astype(jnp.bfloat16)
        stats.append(lse)
    if two:
        own_stats[...] = kept
    store_guest(ret, 0, heads, None, stats)


def audio_kernel(heads, me, start, count, own, own_stats, rx, rz, out):
    me = me[0]
    chip = me // 2
    step = 1 - 2 * (chip % 2)
    cx, cz = chip + step, chip - step
    lo, hi = start[0], start[0] + count[0]

    def reaches(c):
        return (2 * c < hi) & (2 * c + 2 > lo)

    tail = pl.ds(heads * HEAD_DIM, HEAD_DIM)
    sx, sz = rx[:, tail].astype(jnp.float32), rz[:, tail].astype(jnp.float32)
    ok_x, ok_z = reaches(cx), reaches(cz)
    for h in range(heads):
        c = head_cols(h)

        def lse_of(st, ok):
            v = st[:, h : h + 1] + st[:, 32 + h : 33 + h] + st[:, 64 + h : 65 + h]
            return jnp.where(ok, v, NEG)

        l0 = own_stats[:, h : h + 1]
        l1, l2 = lse_of(sx, ok_x), lse_of(sz, ok_z)
        m = jnp.maximum(l0, jnp.maximum(l1, l2))
        w0, w1, w2 = jnp.exp2(l0 - m), jnp.exp2(l1 - m), jnp.exp2(l2 - m)
        r = 1.0 / (w0 + w1 + w2)
        acc = own[:, c] * (w0 * r)
        acc = acc + rx[:, c].astype(jnp.float32) * (w1 * r)
        acc = acc + rz[:, c].astype(jnp.float32) * (w2 * r)
        out[:, c] = acc.astype(jnp.bfloat16)


def video_kernel(heads, me, start, count, q, k0, k1, k2, k3, k4, k5, v0, v1, v2, v3, v4, v5, out):
    me = me[0]
    chip, core = me // 2, me % 2
    x = chip % 2
    lo, hi = start[0], start[0] + count[0]
    far = jnp.where(core == 0, me - 1, me + 1)
    zid = jnp.where(x == 0, me - 2, me + 2)
    by_x = x != core
    never = -1000
    ids = [me, me ^ 1, me ^ 2, jnp.where(by_x, far, never), zid, jnp.where(by_x, never, far)]
    keys = k0.shape[0]
    lane = lanes((1, 2 * keys))
    bias = []
    for j in range(3):
        a, b = ids[2 * j], ids[2 * j + 1]
        block = jnp.where(lane < keys, a, b)
        bias.append(jnp.where((block >= lo) & (block < hi), 0.0, NEG))
    ks, vs = (k0, k1, k2, k3, k4, k5), (v0, v1, v2, v3, v4, v5)
    for h in range(heads):
        c = head_cols(h)
        qh = q[:, c]
        ts = []
        for j in range(3):
            kk = jnp.concatenate([ks[2 * j][:, c], ks[2 * j + 1][:, c]], axis=0)
            ts.append(nt(qh, kk) * SCALE + bias[j])
        m = jnp.max(jnp.maximum(jnp.maximum(ts[0], ts[1]), ts[2]), axis=-1, keepdims=True)
        ps = [jnp.exp2(t - m) for t in ts]
        total = jnp.sum(ps[0] + ps[1] + ps[2], axis=-1, keepdims=True)
        acc = 0.0
        for j in range(3):
            vv = jnp.concatenate([vs[2 * j][:, c], vs[2 * j + 1][:, c]], axis=0)
            acc = acc + nn(ps[j].astype(jnp.bfloat16), vv)
        out[:, c] = (acc / total).astype(jnp.bfloat16)


def call(kernel, outs, n_smem, n_vmem):
    return pl.pallas_call(
        kernel,
        out_shape=outs,
        in_specs=[SMEM] * n_smem + [VMEM] * n_vmem,
        out_specs=jax.tree.map(lambda _: VMEM, outs),
    )


def on_device(n, vq, vk, vv, aq, ak, av, v_start, v_count, a_start, a_count):
    rows, features = aq.shape
    heads = features // HEAD_DIM

    def move(x, pairs):
        return lax.ppermute(x, "seq", pairs)

    across = pairs_of(n, lambda s: s ^ 2)
    mates = pairs_of(n, lambda s: s ^ 1)
    along = pairs_of(n, lambda s: s - 4 if s & 2 else s + 4)
    diagonal = pairs_of(n, lambda s: s + 2 if s & 2 else s - 2)
    far_x = pairs_of(n, lambda s: s ^ 1 if s % 4 in (0, 3) else None)
    far_z = pairs_of(n, lambda s: s ^ 1 if s % 4 in (1, 2) else None)

    me = lax.axis_index("seq").astype(jnp.int32).reshape(1)
    code = a_start * 8 + a_count

    xq = move(aq, across)
    x_code = move(code, across)
    z_code = move(code, diagonal)
    xk = move(ak, across)
    xv = move(av, across)
    mk, mv = move(vk, mates), move(vv, mates)
    pk, pv = move(ak, mates), move(av, mates)
    zq = move(xq, along)

    f32, bf16 = jnp.float32, jnp.bfloat16
    ret_shape = jax.ShapeDtypeStruct((rows, features + HEAD_DIM), bf16)
    own, own_stats, ret_x = call(
        functools.partial(guests_kernel, heads, n, True),
        (
            jax.ShapeDtypeStruct((rows, features), f32),
            jax.ShapeDtypeStruct((rows, HEAD_DIM), f32),
            ret_shape,
        ),
        4,
        6,
    )(me, a_start, a_count, x_code, aq, xq, vk, mk, vv, mv)
    got_x = move(ret_x, across)
    zk = move(xk, along)
    (ret_z,) = call(functools.partial(guests_kernel, heads, n, False), (ret_shape,), 2, 5)(
        me, z_code, zq, vk, mk, vv, mv
    )
    got_z = move(ret_z, diagonal)
    zv = move(xv, along)
    fxk, fxv = move(xk, far_x), move(xv, far_x)
    fzk, fzv = move(zk, far_z), move(zv, far_z)
    (audio,) = call(
        functools.partial(audio_kernel, heads), (jax.ShapeDtypeStruct(aq.shape, bf16),), 3, 4
    )(me, a_start, a_count, own, own_stats, got_x, got_z)
    (video,) = call(
        functools.partial(video_kernel, heads), (jax.ShapeDtypeStruct(vq.shape, bf16),), 3, 13
    )(me, v_start, v_count, vq, ak, pk, xk, fxk, zk, fzk, av, pv, xv, fxv, zv, fzv)
    return video, audio


def solution(mesh):
    rows = P(("groups", "seq"), None)
    each = P(("groups", "seq"))
    return jax.shard_map(
        functools.partial(on_device, mesh.shape["seq"]),
        mesh=mesh,
        in_specs=(rows,) * 6 + (each,) * 4,
        out_specs=(rows, rows),
        check_vma=False,
    )
```
